32 devices in a mesh: seq: 8 (over z, x), head: 4 (over y, core).
Axes of the slice: x: 2, y: 2, z: 4, core: 2. Of those that a mesh axis runs over, the one named last changes fastest.
Arguments:
- query: bfloat16 [1024, 16, 576], P('seq', 'head'), may hold values from -48 to 48
- latents: bfloat16 [1024, 576], P('seq'), may hold values from -6 to 6
- out_grad: bfloat16 [1024, 16, 512], P('seq', 'head'), may hold values from -6 to 6
- saved_out: bfloat16 [1024, 16, 512], P('seq', 'head'), may hold values from -6 to 6
- first_key: int32 [1024], P('seq'), may hold values from 0 to 1022, as said below
Outputs:
- query_grad: float32 [1024, 16, 576], P('seq', 'head')
- latent_grad: float32 [1024, 576], P(('seq', 'head'))
The draws below stay inside these ranges and needn't reach their ends.
Inputs may be any that keep to these rules, and one draw needn't show every extreme that they name: first_key[i] <= i - 1 for i >= 1, first_key[0] = 0, and first_key[i] >= i - 512; the lower bound is met at the first position of every block of 128 from position 512 on.
All inputs are finite; a program needn't handle non-finite values.
Results may differ from the reference program's by a relative error of at most 0.0039.
Values may be sent and summed in bfloat16 or wider, within the bound.
A program may use at most 64 MiB of HBM per device.

```python
import jax
import jax.numpy as jnp
from jax import lax

VAL = 512
QK_HEAD = 192
STEPS = 5
Q_DEV = 128
LAT = 576
HEADS = 16
TOKENS = 1024
N_SEQ = 8


def latent_pair(key):
    latent_key = jax.random.fold_in(key, 11)
    query_key = jax.random.fold_in(key, 12)
    latents = jnp.clip(jax.random.normal(latent_key, (TOKENS, LAT), jnp.float32), -6.0, 6.0)
    queries = jnp.clip(jax.random.normal(query_key, (TOKENS, HEADS, LAT), jnp.float32), -6.0, 6.0)
    return (queries, latents)


def draw_query(key, part):
    return latent_pair(key)[0].astype(jnp.bfloat16)


def draw_latents(key, part):
    return latent_pair(key)[1].astype(jnp.bfloat16)


def draw_first_key(key, part):
    positions = jnp.arange(TOKENS, dtype=jnp.int32)
    reach = jax.random.randint(jax.random.fold_in(key, 21), (TOKENS,), 1, (STEPS - 1) * Q_DEV + 1, dtype=jnp.int32)
    reach = jnp.where(positions % Q_DEV == 0, (STEPS - 1) * Q_DEV, reach)
    return jnp.maximum(positions - reach, 0).astype(jnp.int32)


def block_scale(key, dims, split, smallest, largest):
    loudness = 1.0
    for dim, blocks in split:
        draws = jax.random.uniform(jax.random.fold_in(jax.random.fold_in(key, 6), dim), (blocks,), jnp.float32, smallest / len(split), largest / len(split))
        loudness = loudness * jnp.repeat(jnp.exp(draws), dims[dim] // blocks).reshape((-1,) + (1,) * (len(dims) - 1 - dim))
    return loudness


def bell_draw(key, dims, width, bound, split=(), held_as=jnp.bfloat16):
    entries = width * jax.random.normal(key, dims, jnp.float32)
    if split:
        entries = entries * block_scale(key, dims, split, -0.22, 0.18)
    return jnp.clip(entries, -bound, bound).astype(held_as)


def setup_inputs(seed: int = 0) -> dict:
    key_of = jax.random.split(jax.random.key(seed), 6)
    return {
        "query": draw_query(jax.random.fold_in(key_of[5], 71), 0),
        "latents": draw_latents(jax.random.fold_in(key_of[5], 71), 0),
        "out_grad": bell_draw(key_of[2], (TOKENS, HEADS, VAL), 1.0, 6.0, ((0, 8), (1, 4))),
        "saved_out": bell_draw(key_of[3], (TOKENS, HEADS, VAL), 1.0, 6.0, ((0, 8), (1, 4))),
        "first_key": draw_first_key(jax.random.fold_in(key_of[5], 71), 0),
    }


def visibility(first, query_start, key_start, rows, heads, keys):
    query_pos = jnp.repeat(query_start + jnp.arange(rows, dtype=jnp.int32), heads)
    first_rows = jnp.repeat(first, heads)
    key_pos = key_start + jnp.arange(keys, dtype=jnp.int32)
    return (key_pos[None, :] >= first_rows[:, None]) & (key_pos[None, :] <= query_pos[:, None])


def attention_grads(queries, window, grads_out, outputs, visible):
    softmax_scale = QK_HEAD ** -0.5
    scores = jnp.dot(queries, window.T, preferred_element_type=jnp.float32) * softmax_scale
    scores = jnp.where(visible, scores, -1e30)
    row_max = jnp.max(scores, axis=1, keepdims=True)
    row_total = jnp.sum(jnp.where(visible, jnp.exp(scores - row_max), 0.0), axis=1, keepdims=True)
    log_norm = row_max + jnp.log(row_total)
    probs = jnp.where(visible, jnp.exp(scores - log_norm), 0.0)
    row_dot = jnp.sum(grads_out.astype(jnp.float32) * outputs.astype(jnp.float32), axis=1, keepdims=True)
    prob_grad = jnp.dot(grads_out, window[:, :VAL].T, preferred_element_type=jnp.float32)
    score_grad = (probs * (prob_grad - row_dot)).astype(jnp.bfloat16)
    probs_low = probs.astype(jnp.bfloat16)
    query_grad = jnp.dot(score_grad, window, preferred_element_type=jnp.float32) * softmax_scale
    contract = (((0,), (0,)), ((), ()))
    latent_grad = lax.dot_general(score_grad, queries, contract, preferred_element_type=jnp.float32) * softmax_scale
    value_grad = lax.dot_general(probs_low, grads_out, contract, preferred_element_type=jnp.float32)
    padding = jnp.zeros((window.shape[0], window.shape[1] - VAL), jnp.float32)
    latent_grad = latent_grad + jnp.concatenate([value_grad, padding], axis=1)
    return query_grad, latent_grad


def reference(query, latents, out_grad, saved_out, first_key):
    span = STEPS * Q_DEV
    lead = (STEPS - 1) * Q_DEV
    padded = jnp.concatenate([jnp.zeros((lead, LAT), latents.dtype), latents], axis=0)

    def per_block(block_index):
        start = (block_index * Q_DEV).astype(jnp.int32)
        queries = lax.dynamic_slice_in_dim(query, start, Q_DEV, 0).reshape(Q_DEV * HEADS, LAT)
        window = lax.dynamic_slice_in_dim(padded, start, span, 0)
        grads_out = lax.dynamic_slice_in_dim(out_grad, start, Q_DEV, 0).reshape(Q_DEV * HEADS, VAL)
        outputs = lax.dynamic_slice_in_dim(saved_out, start, Q_DEV, 0).reshape(Q_DEV * HEADS, VAL)
        first = lax.dynamic_slice_in_dim(first_key, start, Q_DEV, 0).astype(jnp.int32)
        visible = visibility(first, start, start - lead, Q_DEV, HEADS, span)
        return attention_grads(queries, window, grads_out, outputs, visible)

    query_parts, latent_parts = lax.map(per_block, jnp.arange(N_SEQ, dtype=jnp.int32))
    query_grad = query_parts.reshape(TOKENS, HEADS, LAT)
    totals = jnp.zeros((lead + TOKENS, LAT), jnp.float32)

    def add_window(block_index, totals):
        start = (block_index * Q_DEV).astype(jnp.int32)
        current = lax.dynamic_slice_in_dim(totals, start, span, 0)
        return lax.dynamic_update_slice_in_dim(totals, current + latent_parts[block_index], start, 0)

    totals = lax.fori_loop(0, N_SEQ, add_window, totals)
    return query_grad, totals[lead:]
```

```python
import functools

import jax
import jax.numpy as jnp
from jax import lax
from jax.experimental import pallas as pl
from jax.experimental.pallas import tpu as pltpu
from jax.sharding import PartitionSpec as P

VAL = 512
QK_HEAD = 192
STEPS = 5
MESH = pl.DeviceIdType.MESH
SCALE = QK_HEAD ** (-0.5)
F32 = jnp.float32
BF16 = jnp.bfloat16


def dot(a, b, ca, cb):
    return lax.dot_general(a, b, (((ca,), (cb,)), ((), ())), preferred_element_type=F32)


def fused_kernel(n_seq, n_head, levels,
                 q_hbm, lat_hbm, g_hbm, o_hbm, first_ref,
                 qg_ref, lg_ref,
                 q_v, g_v, o_v, gh_v, win, s_v, dp_v, ds_v, accs, wires, recvs,
                 wire_seq, recv_seq,
                 in_sem, gs_sem, gr_sem, hs_sem, hr_sem, rs_sem, rr_sem):
    heads, width, rows = q_v.shape
    back = STEPS - 1
    part = width // n_head
    s = lax.axis_index("seq")
    h = lax.axis_index("head")
    bits = [(h // (1 << t)) % 2 for t in range(levels)]
    partners = [h + (1 << t) * (1 - 2 * bits[t]) for t in range(levels)]

    loads = [
        pltpu.make_async_copy(lat_hbm, win.at[0], in_sem.at[0]),
        pltpu.make_async_copy(q_hbm, q_v, in_sem.at[1]),
        pltpu.make_async_copy(g_hbm, g_v, in_sem.at[2]),
        pltpu.make_async_copy(o_hbm, o_v, in_sem.at[3]),
    ]
    for copy in loads:
        copy.start()

    barrier = pltpu.get_barrier_semaphore()

    def greet(dev):
        pl.semaphore_signal(barrier, inc=1, device_id=dev, device_id_type=MESH)

    for t in range(levels):
        greet((s, partners[t]))
    for k in range(1, STEPS):
        @pl.when(s >= k)
        def _():
            greet((s - k, h))

        @pl.when(s + k < n_seq)
        def _():
            greet((s + k, h))
    peers = levels
    for k in range(1, min(STEPS, n_seq)):
        peers = peers + lax.div(s - k + n_seq, n_seq) + lax.div(2 * n_seq - 1 - s - k, n_seq)
    pl.semaphore_wait(barrier, peers)

    def chunk(q):
        return pl.ds(pl.multiple_of(q * part, 16), part)

    def seq_send(k):
        return pltpu.make_async_remote_copy(
            src_ref=lat_hbm.at[chunk(h)], dst_ref=win.at[k, chunk(h)],
            send_sem=gs_sem.at[k - 1, 0], recv_sem=gr_sem.at[k - 1, 0],
            device_id=(s + k, h), device_id_type=MESH)

    for k in range(1, STEPS):
        @pl.when(s + k < n_seq)
        def _():
            seq_send(k).start()

    plan = []
    slot = 1
    for t in range(levels - 1, -1, -1):
        low = 1 << (t + 1)
        stage = []
        for m in range(n_head // low):
            stage.append((slot, h % low + low * m))
            slot += 1
        plan.append((t, stage))

    def pass_on(k, t, sl, q):
        return pltpu.make_async_remote_copy(
            src_ref=win.at[k, chunk(q)], dst_ref=win.at[k, chunk(q)],
            send_sem=gs_sem.at[k - 1, sl], recv_sem=gr_sem.at[k - 1, sl],
            device_id=(s, partners[t]), device_id_type=MESH)

    for k in range(1, STEPS):
        @pl.when(s < k)
        def _():
            win[k] = jnp.zeros((width, rows), BF16)

    first = first_ref[...]
    query_pos = s * rows + lax.broadcasted_iota(jnp.int32, (1, rows), 1)

    def score_block(k):
        keys = win[k].T
        key_pos = (s - k) * rows + lax.broadcasted_iota(jnp.int32, (rows, rows), 0)
        visible = (key_pos >= first) & (key_pos <= query_pos)
        best = []
        for hd in range(heads):
            cols = pl.ds(hd * rows, rows)
            sc = dot(keys, q_v[hd], 1, 0) * SCALE
            sc = jnp.where(visible, sc, -1e30)
            s_v[k, :, cols] = sc
            best.append(jnp.max(sc, axis=0, keepdims=True))
        dp_v[k] = dot(keys[:, :VAL], gh_v[...], 1, 1)
        return jnp.concatenate(best, axis=1)

    for copy in loads[1:]:
        copy.wait()
    dots = []
    for hd in range(heads):
        g_h = g_v[:, hd, :]
        gh_v[pl.ds(hd * rows, rows), :] = g_h
        prod = jnp.sum(g_h.astype(F32) * o_v[:, hd, :].astype(F32), axis=1, keepdims=True)
        dots.append(jnp.broadcast_to(prod, (rows, rows)).T[0:1, :])
    row_dot = jnp.concatenate(dots, axis=1)
    loads[0].wait()
    row_max = score_block(0)

    for level in range(len(plan) + 1):
        for k in range(1, STEPS):
            @pl.when(s >= k)
            def _():
                if level == 0:
                    seq_send(k).wait_recv()
                else:
                    t, stage = plan[level - 1]
                    for sl, q in stage:
                        pass_on(k, t, sl, q).wait_recv()
                if level < len(plan):
                    t, stage = plan[level]
                    for sl, q in stage:
                        pass_on(k, t, sl, q).start()
            if level == len(plan):
                row_max = jnp.maximum(row_max, score_block(k))

    total = jnp.zeros_like(row_max)
    for k in range(STEPS):
        total += jnp.sum(jnp.exp(s_v[k] - row_max), axis=0, keepdims=True)
    log_norm = row_max + jnp.log(total)

    grads = gh_v[...]
    queries = jnp.concatenate([q_v[hd] for hd in range(heads)], axis=1)

    def head_copy(t, k, m):
        src = 2 * m + 1 - bits[t]
        return pltpu.make_async_remote_copy(
            src_ref=wires[t].at[k, src], dst_ref=recvs[t].at[k, m],
            send_sem=hs_sem[t].at[k, m], recv_sem=hr_sem[t].at[k, m],
            device_id=(s, partners[t]), device_id_type=MESH)

    def kept(t):
        return n_head >> (t + 1)

    order = list(range(back, -1, -1))
    for k in order:
        probs = jnp.exp(s_v[k] - log_norm)
        score_grad = (probs * (dp_v[k] - row_dot)).astype(BF16)
        ds_v[pl.ds(k * rows, rows), :] = score_grad
        lat = dot(score_grad, queries, 1, 1) * SCALE
        val = dot(probs.astype(BF16), grads, 1, 0)
        lat = jnp.concatenate([lat[:, :VAL] + val, lat[:, VAL:]], axis=1)
        lat = lat.reshape(n_head, rows // n_head, width)
        accs[0][k] = lat
        wires[0][k] = lat.astype(BF16)
        for m in range(kept(0)):
            head_copy(0, k, m).start()

    def seq_copy(k):
        return pltpu.make_async_remote_copy(
            src_ref=wire_seq.at[k - 1], dst_ref=recv_seq.at[k - 1],
            send_sem=rs_sem.at[k - 1], recv_sem=rr_sem.at[k - 1],
            device_id=(s - k, h), device_id_type=MESH)

    window = jnp.concatenate([win[k] for k in range(STEPS)], axis=1)

    def query_grad(hd):
        qg_ref[hd] = dot(window, ds_v[:, pl.ds(hd * rows, rows)], 1, 0) * SCALE

    done = 0
    for t in range(levels):
        if done < heads:
            query_grad(done)
            done += 1
        for k in order:
            for m in range(kept(t)):
                head_copy(t, k, m).wait_recv()
                new = accs[t][k, 2 * m + bits[t]] + recvs[t][k, m].astype(F32)
                accs[t + 1][k, m] = new
                if t + 1 < levels:
                    wires[t + 1][k, m] = new.astype(BF16)
                elif k:
                    wire_seq[k - 1] = new.astype(BF16)
            if t + 1 < levels:
                for m in range(kept(t + 1)):
                    head_copy(t + 1, k, m).start()
            elif k:
                @pl.when(s >= k)
                def _():
                    seq_copy(k).start()
    while done < heads:
        query_grad(done)
        done += 1

    lg_ref[...] = accs[levels][0, 0]
    for k in range(1, STEPS):
        @pl.when(s + k < n_seq)
        def _():
            seq_copy(k).wait_recv()
            lg_ref[...] += recv_seq[k - 1].astype(F32)

    for k in range(1, STEPS):
        @pl.when(s + k < n_seq)
        def _():
            seq_send(k).wait_send()

        @pl.when(s >= k)
        def _():
            for t, stage in plan:
                for sl, q in stage:
                    pass_on(k, t, sl, q).wait_send()
            seq_copy(k).wait_send()
    for t in range(levels):
        for k in order:
            for m in range(kept(t)):
                head_copy(t, k, m).wait_send()


def fused_body(n_seq, n_head, query, latents, out_grad, saved_out, first_key):
    rows, heads, width = query.shape
    levels = n_head.bit_length() - 1
    piece = rows // n_head
    cells = rows * heads
    hbm = pl.BlockSpec(memory_space=pltpu.MemorySpace.HBM)
    vmem = pl.BlockSpec(memory_space=pltpu.VMEM)
    dma = pltpu.SemaphoreType.DMA
    scratch = [
        pltpu.VMEM((heads, width, rows), BF16),
        pltpu.VMEM((rows, heads, VAL), BF16),
        pltpu.VMEM((rows, heads, VAL), BF16),
        pltpu.VMEM((cells, VAL), BF16),
        pltpu.VMEM((STEPS, width, rows), BF16),
        pltpu.VMEM((STEPS, rows, cells), F32),
        pltpu.VMEM((STEPS, rows, cells), F32),
        pltpu.VMEM((STEPS * rows, cells), BF16),
        [pltpu.VMEM((STEPS, n_head >> t, piece, width), F32) for t in range(levels + 1)],
        [pltpu.VMEM((STEPS, n_head >> t, piece, width), BF16) for t in range(levels)],
        [pltpu.VMEM((STEPS, n_head >> (t + 1), piece, width), BF16) for t in range(levels)],
        pltpu.VMEM((STEPS - 1, piece, width), BF16),
        pltpu.VMEM((STEPS - 1, piece, width), BF16),
        dma((4,)),
        dma((STEPS - 1, n_head)),
        dma((STEPS - 1, n_head)),
        [dma((STEPS, n_head >> (t + 1))) for t in range(levels)],
        [dma((STEPS, n_head >> (t + 1))) for t in range(levels)],
        dma((STEPS - 1,)),
        dma((STEPS - 1,)),
    ]
    query_grad, latent_grad = pl.pallas_call(
        functools.partial(fused_kernel, n_seq, n_head, levels),
        out_shape=(
            jax.ShapeDtypeStruct((heads, width, rows), F32),
            jax.ShapeDtypeStruct((piece, width), F32),
        ),
        in_specs=[hbm, hbm, hbm, hbm, vmem],
        out_specs=(vmem, vmem),
        scratch_shapes=scratch,
        compiler_params=pltpu.CompilerParams(
            collective_id=0, has_side_effects=True, vmem_limit_bytes=48 * 1024 * 1024
        ),
    )(
        jnp.transpose(query, (1, 2, 0)),
        latents.T,
        out_grad,
        saved_out,
        first_key.reshape(1, rows),
    )
    return jnp.transpose(query_grad, (2, 0, 1)), latent_grad


def shifted(block, axis, distance):
    devices = range(lax.axis_size(axis))
    route = [(i - distance, i) for i in devices if i - distance in devices]
    return lax.ppermute(block, axis, route)


def visibility(first, query_start, key_start, rows, heads, keys):
    query_pos = jnp.repeat(query_start + jnp.arange(rows, dtype=jnp.int32), heads)
    first_rows = jnp.repeat(first, heads)
    key_pos = key_start + jnp.arange(keys, dtype=jnp.int32)
    return (key_pos[None, :] >= first_rows[:, None]) & (key_pos[None, :] <= query_pos[:, None])


def attention_grads(queries, window, grads_out, outputs, visible):
    scores = jnp.dot(queries, window.T, preferred_element_type=F32) * SCALE
    scores = jnp.where(visible, scores, -1e30)
    row_max = jnp.max(scores, axis=1, keepdims=True)
    row_total = jnp.sum(jnp.where(visible, jnp.exp(scores - row_max), 0.0), axis=1, keepdims=True)
    log_norm = row_max + jnp.log(row_total)
    probs = jnp.where(visible, jnp.exp(scores - log_norm), 0.0)
    row_dot = jnp.sum(grads_out.astype(F32) * outputs.astype(F32), axis=1, keepdims=True)
    prob_grad = jnp.dot(grads_out, window[:, :VAL].T, preferred_element_type=F32)
    score_grad = (probs * (prob_grad - row_dot)).astype(BF16)
    query_grad = jnp.dot(score_grad, window, preferred_element_type=F32) * SCALE
    latent_grad = dot(score_grad, queries, 0, 0) * SCALE
    value_grad = dot(probs.astype(BF16), grads_out, 0, 0)
    padding = jnp.zeros((window.shape[0], window.shape[1] - VAL), F32)
    return query_grad, latent_grad + jnp.concatenate([value_grad, padding], axis=1)


def plain_body(query, latents, out_grad, saved_out, first_key):
    rows, heads, width = query.shape
    here = lax.axis_index("seq")
    blocks = [latents]
    for _ in range(STEPS - 1):
        blocks.append(shifted(blocks[-1], "seq", 1))
    window = jnp.concatenate(blocks[::-1], axis=0)
    start = here * rows
    visible = visibility(
        first_key, start, start - (STEPS - 1) * rows, rows, heads, STEPS * rows
    )
    query_grad, latent_grad = attention_grads(
        query.reshape(rows * heads, width),
        window,
        out_grad.reshape(rows * heads, VAL),
        saved_out.reshape(rows * heads, VAL),
        visible,
    )
    pieces = latent_grad.reshape(STEPS, rows, width)
    carried = pieces[0]
    for hop in range(1, STEPS):
        carried = shifted(carried, "seq", -1) + pieces[hop]
    carried = lax.psum_scatter(carried, "head", scatter_dimension=0, tiled=True)
    return query_grad.reshape(rows, heads, width), carried


def solution(mesh):
    n_seq, n_head = mesh.shape["seq"], mesh.shape["head"]

    def body(query, latents, out_grad, saved_out, first_key):
        rows, heads, width = query.shape
        fits = n_head & (n_head - 1) == 0 and n_head > 1
        fits = fits and rows % (16 * n_head) == 0 and width % (16 * n_head) == 0
        if fits:
            return fused_body(n_seq, n_head, query, latents, out_grad, saved_out, first_key)
        return plain_body(query, latents, out_grad, saved_out, first_key)

    in_specs = (
        P("seq", "head", None),
        P("seq", None),
        P("seq", "head", None),
        P("seq", "head", None),
        P("seq"),
    )
    out_specs = (P("seq", "head", None), P(("seq", "head"), None))
    return jax.shard_map(body, mesh=mesh, in_specs=in_specs, out_specs=out_specs, check_vma=False)
```

```python
import functools

import jax
import jax.numpy as jnp
from jax import lax
from jax.experimental import pallas as pl
from jax.experimental.pallas import tpu as pltpu
from jax.sharding import PartitionSpec as P

VAL = 512
QK_HEAD = 192
STEPS = 5
MESH = pl.DeviceIdType.MESH
SCALE = QK_HEAD ** (-0.5)
F32 = jnp.float32
BF16 = jnp.bfloat16


def dot(a, b, ca, cb):
    return lax.dot_general(a, b, (((ca,), (cb,)), ((), ())), preferred_element_type=F32)


def fused_kernel(n_seq, n_head, levels,
                 q_hbm, lat_hbm, g_hbm, o_hbm, first_hbm,
                 qg_ref, lg_ref,
                 q_v, g_v, o_v, first_v, gh_v, win, s_v, dp_v, ds_v, accs, wires, recvs,
                 wire_seq, recv_seq,
                 in_sem, gs_sem, gr_sem, hs_sem, hr_sem, rs_sem, rr_sem):
    heads, width, rows = q_v.shape
    back = STEPS - 1
    part = width // n_head
    s = lax.axis_index("seq")
    h = lax.axis_index("head")
    bits = [(h // (1 << t)) % 2 for t in range(levels)]
    partners = [h + (1 << t) * (1 - 2 * bits[t]) for t in range(levels)]

    loads = [
        pltpu.make_async_copy(lat_hbm, win.at[0], in_sem.at[0]),
        pltpu.make_async_copy(q_hbm, q_v, in_sem.at[1]),
        pltpu.make_async_copy(g_hbm, g_v, in_sem.at[2]),
        pltpu.make_async_copy(o_hbm, o_v, in_sem.at[3]),
        pltpu.make_async_copy(first_hbm, first_v, in_sem.at[4]),
    ]
    for copy in loads:
        copy.start()

    barrier = pltpu.get_barrier_semaphore()

    def greet(dev):
        pl.semaphore_signal(barrier, inc=1, device_id=dev, device_id_type=MESH)

    for t in range(levels):
        greet((s, partners[t]))
    for k in range(1, STEPS):
        @pl.when(s >= k)
        def _():
            greet((s - k, h))

        @pl.when(s + k < n_seq)
        def _():
            greet((s + k, h))
    peers = levels
    for k in range(1, min(STEPS, n_seq)):
        peers = peers + lax.div(s - k + n_seq, n_seq) + lax.div(2 * n_seq - 1 - s - k, n_seq)
    pl.semaphore_wait(barrier, peers)

    def chunk(q):
        return pl.ds(pl.multiple_of(q * part, 16), part)

    def seq_send(k):
        return pltpu.make_async_remote_copy(
            src_ref=lat_hbm.at[chunk(h)], dst_ref=win.at[k, chunk(h)],
            send_sem=gs_sem.at[k - 1, 0], recv_sem=gr_sem.at[k - 1, 0],
            device_id=(s + k, h), device_id_type=MESH)

    for k in range(1, STEPS):
        @pl.when(s + k < n_seq)
        def _():
            seq_send(k).start()

    plan = []
    slot = 1
    for t in range(levels - 1, -1, -1):
        low = 1 << (t + 1)
        stage = []
        for m in range(n_head // low):
            stage.append((slot, h % low + low * m))
            slot += 1
        plan.append((t, stage))

    def pass_on(k, t, sl, q):
        return pltpu.make_async_remote_copy(
            src_ref=win.at[k, chunk(q)], dst_ref=win.at[k, chunk(q)],
            send_sem=gs_sem.at[k - 1, sl], recv_sem=gr_sem.at[k - 1, sl],
            device_id=(s, partners[t]), device_id_type=MESH)

    for k in range(1, STEPS):
        @pl.when(s < k)
        def _():
            win[k] = jnp.zeros((width, rows), BF16)

    query_pos = s * rows + lax.broadcasted_iota(jnp.int32, (1, rows), 1)

    def score_block(k):
        keys = win[k].T
        key_pos = (s - k) * rows + lax.broadcasted_iota(jnp.int32, (rows, rows), 0)
        visible = (key_pos >= first) & (key_pos <= query_pos)
        best = []
        for hd in range(heads):
            cols = pl.ds(hd * rows, rows)
            sc = dot(keys, q_v[hd], 1, 0) * SCALE
            sc = jnp.where(visible, sc, -1e30)
            s_v[k, :, cols] = sc
            best.append(jnp.max(sc, axis=0, keepdims=True))
        dp_v[k] = dot(keys[:, :VAL], gh_v[...], 1, 1)
        return jnp.concatenate(best, axis=1)

    for copy in loads[1:]:
        copy.wait()
    first = first_v[...]
    dots = []
    for hd in range(heads):
        g_h = g_v[:, hd, :]
        gh_v[pl.ds(hd * rows, rows), :] = g_h
        prod = jnp.sum(g_h.astype(F32) * o_v[:, hd, :].astype(F32), axis=1, keepdims=True)
        dots.append(jnp.broadcast_to(prod, (rows, rows)).T[0:1, :])
    row_dot = jnp.concatenate(dots, axis=1)
    loads[0].wait()
    row_max = score_block(0)

    arrivals = [(k + 1.5 * level, level, k)
                for level in range(len(plan) + 1) for k in range(1, STEPS)]
    for _, level, k in sorted(arrivals):
        @pl.when(s >= k)
        def _():
            if level == 0:
                seq_send(k).wait_recv()
            else:
                t, stage = plan[level - 1]
                for sl, q in stage:
                    pass_on(k, t, sl, q).wait_recv()
            if level < len(plan):
                t, stage = plan[level]
                for sl, q in stage:
                    pass_on(k, t, sl, q).start()
        if level == len(plan):
            row_max = jnp.maximum(row_max, score_block(k))

    total = jnp.zeros_like(row_max)
    for k in range(STEPS):
        total += jnp.sum(jnp.exp(s_v[k] - row_max), axis=0, keepdims=True)
    log_norm = row_max + jnp.log(total)

    grads = gh_v[...]
    queries = jnp.concatenate([q_v[hd] for hd in range(heads)], axis=1)

    def head_copy(t, k, m):
        src = 2 * m + 1 - bits[t]
        return pltpu.make_async_remote_copy(
            src_ref=wires[t].at[k, src], dst_ref=recvs[t].at[k, m],
            send_sem=hs_sem[t].at[k, m], recv_sem=hr_sem[t].at[k, m],
            device_id=(s, partners[t]), device_id_type=MESH)

    def kept(t):
        return n_head >> (t + 1)

    order = list(range(back, -1, -1))

    def latent_grad(k):
        probs = jnp.exp(s_v[k] - log_norm)
        score_grad = (probs * (dp_v[k] - row_dot)).astype(BF16)
        ds_v[pl.ds(k * rows, rows), :] = score_grad
        lat = dot(score_grad, queries, 1, 1) * SCALE
        val = dot(probs.astype(BF16), grads, 1, 0)
        lat = jnp.concatenate([lat[:, :VAL] + val, lat[:, VAL:]], axis=1)
        lat = lat.reshape(n_head, rows // n_head, width)
        accs[0][k] = lat
        wires[0][k] = lat.astype(BF16)
        for m in range(kept(0)):
            head_copy(0, k, m).start()

    def seq_copy(k):
        return pltpu.make_async_remote_copy(
            src_ref=wire_seq.at[k - 1], dst_ref=recv_seq.at[k - 1],
            send_sem=rs_sem.at[k - 1], recv_sem=rr_sem.at[k - 1],
            device_id=(s - k, h), device_id_type=MESH)

    window = jnp.concatenate([win[k] for k in range(STEPS)], axis=1)

    def query_grad(hd):
        qg_ref[hd] = dot(window, ds_v[:, pl.ds(hd * rows, rows)], 1, 0) * SCALE

    def halve(t, k):
        for m in range(kept(t)):
            head_copy(t, k, m).wait_recv()
            new = accs[t][k, 2 * m + bits[t]] + recvs[t][k, m].astype(F32)
            accs[t + 1][k, m] = new
            if t + 1 < levels:
                wires[t + 1][k, m] = new.astype(BF16)
                head_copy(t + 1, k, m // 2).start() if m % 2 else None
            elif k:
                wire_seq[k - 1] = new.astype(BF16)
        if t + 1 == levels and k:
            @pl.when(s >= k)
            def _():
                seq_copy(k).start()

    work = [(i, 0, latent_grad, (k,)) for i, k in enumerate(order)]
    for t in range(levels):
        work += [(i + 3.5 + 5 * t, 2, halve, (t, k)) for i, k in enumerate(order)]
    work += [(len(order) + 2.5 + i, 1, query_grad, (i,)) for i in range(heads)]
    for _, _, step, operands in sorted(work, key=lambda item: item[:2]):
        step(*operands)

    lg_ref[...] = accs[levels][0, 0]
    for k in range(1, STEPS):
        @pl.when(s + k < n_seq)
        def _():
            seq_copy(k).wait_recv()
            lg_ref[...] += recv_seq[k - 1].astype(F32)

    for k in range(1, STEPS):
        @pl.when(s + k < n_seq)
        def _():
            seq_send(k).wait_send()

        @pl.when(s >= k)
        def _():
            for t, stage in plan:
                for sl, q in stage:
                    pass_on(k, t, sl, q).wait_send()
            seq_copy(k).wait_send()
    for t in range(levels):
        for k in order:
            for m in range(kept(t)):
                head_copy(t, k, m).wait_send()


def fused_body(n_seq, n_head, query, latents, out_grad, saved_out, first_key):
    rows, heads, width = query.shape
    levels = n_head.bit_length() - 1
    piece = rows // n_head
    cells = rows * heads
    hbm = pl.BlockSpec(memory_space=pltpu.MemorySpace.HBM)
    vmem = pl.BlockSpec(memory_space=pltpu.VMEM)
    dma = pltpu.SemaphoreType.DMA
    scratch = [
        pltpu.VMEM((heads, width, rows), BF16),
        pltpu.VMEM((rows, heads, VAL), BF16),
        pltpu.VMEM((rows, heads, VAL), BF16),
        pltpu.VMEM((1, rows), jnp.int32),
        pltpu.VMEM((cells, VAL), BF16),
        pltpu.VMEM((STEPS, width, rows), BF16),
        pltpu.VMEM((STEPS, rows, cells), F32),
        pltpu.VMEM((STEPS, rows, cells), F32),
        pltpu.VMEM((STEPS * rows, cells), BF16),
        [pltpu.VMEM((STEPS, n_head >> t, piece, width), F32) for t in range(levels + 1)],
        [pltpu.VMEM((STEPS, n_head >> t, piece, width), BF16) for t in range(levels)],
        [pltpu.VMEM((STEPS, n_head >> (t + 1), piece, width), BF16) for t in range(levels)],
        pltpu.VMEM((STEPS - 1, piece, width), BF16),
        pltpu.VMEM((STEPS - 1, piece, width), BF16),
        dma((5,)),
        dma((STEPS - 1, n_head)),
        dma((STEPS - 1, n_head)),
        [dma((STEPS, n_head >> (t + 1))) for t in range(levels)],
        [dma((STEPS, n_head >> (t + 1))) for t in range(levels)],
        dma((STEPS - 1,)),
        dma((STEPS - 1,)),
    ]
    query_grad, latent_grad = pl.pallas_call(
        functools.partial(fused_kernel, n_seq, n_head, levels),
        out_shape=(
            jax.ShapeDtypeStruct((heads, width, rows), F32),
            jax.ShapeDtypeStruct((piece, width), F32),
        ),
        in_specs=[hbm] * 5,
        out_specs=(vmem, vmem),
        scratch_shapes=scratch,
        compiler_params=pltpu.CompilerParams(
            collective_id=0, has_side_effects=True, vmem_limit_bytes=40 * 1024 * 1024
        ),
    )(
        *(
            pltpu.with_memory_space_constraint(x, pltpu.MemorySpace.HBM)
            for x in (
                jnp.transpose(query, (1, 2, 0)),
                latents.T,
                out_grad,
                saved_out,
                first_key.reshape(1, rows),
            )
        ),
    )
    return jnp.transpose(query_grad, (2, 0, 1)), latent_grad


def shifted(block, axis, distance):
    devices = range(lax.axis_size(axis))
    route = [(i - distance, i) for i in devices if i - distance in devices]
    return lax.ppermute(block, axis, route)


def visibility(first, query_start, key_start, rows, heads, keys):
    query_pos = jnp.repeat(query_start + jnp.arange(rows, dtype=jnp.int32), heads)
    first_rows = jnp.repeat(first, heads)
    key_pos = key_start + jnp.arange(keys, dtype=jnp.int32)
    return (key_pos[None, :] >= first_rows[:, None]) & (key_pos[None, :] <= query_pos[:, None])


def attention_grads(queries, window, grads_out, outputs, visible):
    scores = jnp.dot(queries, window.T, preferred_element_type=F32) * SCALE
    scores = jnp.where(visible, scores, -1e30)
    row_max = jnp.max(scores, axis=1, keepdims=True)
    row_total = jnp.sum(jnp.where(visible, jnp.exp(scores - row_max), 0.0), axis=1, keepdims=True)
    log_norm = row_max + jnp.log(row_total)
    probs = jnp.where(visible, jnp.exp(scores - log_norm), 0.0)
    row_dot = jnp.sum(grads_out.astype(F32) * outputs.astype(F32), axis=1, keepdims=True)
    prob_grad = jnp.dot(grads_out, window[:, :VAL].T, preferred_element_type=F32)
    score_grad = (probs * (prob_grad - row_dot)).astype(BF16)
    query_grad = jnp.dot(score_grad, window, preferred_element_type=F32) * SCALE
    latent_grad = dot(score_grad, queries, 0, 0) * SCALE
    value_grad = dot(probs.astype(BF16), grads_out, 0, 0)
    padding = jnp.zeros((window.shape[0], window.shape[1] - VAL), F32)
    return query_grad, latent_grad + jnp.concatenate([value_grad, padding], axis=1)


def plain_body(query, latents, out_grad, saved_out, first_key):
    rows, heads, width = query.shape
    here = lax.axis_index("seq")
    blocks = [latents]
    for _ in range(STEPS - 1):
        blocks.append(shifted(blocks[-1], "seq", 1))
    window = jnp.concatenate(blocks[::-1], axis=0)
    start = here * rows
    visible = visibility(
        first_key, start, start - (STEPS - 1) * rows, rows, heads, STEPS * rows
    )
    query_grad, latent_grad = attention_grads(
        query.reshape(rows * heads, width),
        window,
        out_grad.reshape(rows * heads, VAL),
        saved_out.reshape(rows * heads, VAL),
        visible,
    )
    pieces = latent_grad.reshape(STEPS, rows, width)
    carried = pieces[0]
    for hop in range(1, STEPS):
        carried = shifted(carried, "seq", -1) + pieces[hop]
    carried = lax.psum_scatter(carried, "head", scatter_dimension=0, tiled=True)
    return query_grad.reshape(rows, heads, width), carried


def solution(mesh):
    n_seq, n_head = mesh.shape["seq"], mesh.shape["head"]

    def body(query, latents, out_grad, saved_out, first_key):
        rows, heads, width = query.shape
        fits = n_head & (n_head - 1) == 0 and n_head > 1
        fits = fits and rows % (16 * n_head) == 0 and width % (16 * n_head) == 0
        if fits:
            return fused_body(n_seq, n_head, query, latents, out_grad, saved_out, first_key)
        return plain_body(query, latents, out_grad, saved_out, first_key)

    in_specs = (
        P("seq", "head", None),
        P("seq", None),
        P("seq", "head", None),
        P("seq", "head", None),
        P("seq"),
    )
    out_specs = (P("seq", "head", None), P(("seq", "head"), None))
    return jax.shard_map(body, mesh=mesh, in_specs=in_specs, out_specs=out_specs, check_vma=False)
```
